32 devices in a mesh: groups: 2 (over x), seq: 16 (over z, y, core).
Axes of the slice: x: 2, y: 2, z: 4, core: 2. Of those that a mesh axis runs over, the one named last changes fastest.
Arguments:
- tokens: bfloat16 [262144, 2048], P(('groups', 'seq')), parts along dimension 0, may hold values from -6 to 6
- right_blocks: bfloat16 [256, 512, 512], P('seq'), may hold values from -0.25 to 0.25
- left_blocks: bfloat16 [512, 256, 256], P('seq'), may hold values from -0.375 to 0.375
- chan_first: bfloat16 [32, 64, 64], replicated, may hold values from -0.75 to 0.75
- chan_second: bfloat16 [64, 32, 32], replicated, may hold values from -1 to 1
Outputs:
- mixed: bfloat16 [262144, 2048], P(('groups', 'seq')), parts along dimension 0
The draws below stay inside these ranges and needn't reach their ends.
There are 2 independent parts, one for each index of `groups`. The reference program is written for one: setup_inputs(seed, part) draws one part's arguments, and reference() takes and returns one part's arrays. A program takes and returns all parts, laid end to end along the dimension named above; an argument that names none is the same for every part. Nothing has to cross between parts.
All inputs are finite; a program needn't handle non-finite values.
Results may differ from the reference program's by a relative error of at most 0.007.
Values may be sent and summed in bfloat16 or wider, within the bound.
A program may use at most 384 MiB of HBM per device.

```python
import jax
import jax.numpy as jnp
from jax import lax

RB = 512
LB = 256
CK = 32
CM = 64
D = 2048
SEQ = 131072


def shard_levels(key, shape, shards, low, largest):
    loudness, own = 1.0, jax.random.fold_in(key, 6)
    for position, shards_of in shards:
        draws = jnp.exp(jax.random.uniform(jax.random.fold_in(own, position), (shards_of,), jnp.float32, low / len(shards), largest / len(shards)))
        loudness = loudness * jnp.repeat(draws, shape[position] // shards_of).reshape([-1 if axis == position else 1 for axis in range(len(shape))])
    return loudness


def bell_draw(stream_key, extent, deviation, bound, cuts=(), kind=jnp.bfloat16):
    level = shard_levels(stream_key, extent, cuts, -0.22, 0.18) if cuts else 1.0
    entries = jax.random.normal(stream_key, extent, jnp.float32) * deviation * level
    return jnp.minimum(jnp.maximum(entries, -bound), bound).astype(kind)


def setup_inputs(seed: int = 0, part: int = 0) -> dict:
    seeds = jax.random.split(jax.random.key(seed), 6)
    part_splits = jax.random.split(jax.random.fold_in(seeds[5], part), 6)
    tokens = bell_draw(part_splits[0], (SEQ, D), 1.0, 6.0, ((0, 16),))
    right_blocks = bell_draw(seeds[1], (LB, RB, RB), RB ** -0.5, 0.25, ((0, 16),))
    left_blocks = bell_draw(seeds[2], (RB, LB, LB), LB ** -0.5, 0.375, ((0, 16),))
    chan_first = bell_draw(seeds[3], (CK, CM, CM), CM ** -0.5, 0.75)
    chan_second = bell_draw(seeds[4], (CM, CK, CK), CK ** -0.5, 1.0)
    return dict(tokens=tokens, right_blocks=right_blocks, left_blocks=left_blocks, chan_first=chan_first, chan_second=chan_second)


def channel_mix(pair):
    block, first_w, second_w = pair
    g = block.reshape(block.shape[0], CK, CM).astype(jnp.float32)
    mid = jnp.einsum('kom,skm->sko', first_w.astype(jnp.float32), g).astype(jnp.bfloat16)
    out = jnp.einsum('mok,skm->som', second_w.astype(jnp.float32), mid.astype(jnp.float32))
    return out.reshape(block.shape[0], CK * CM).astype(jnp.bfloat16)


def reference(tokens, right_blocks, left_blocks, chan_first, chan_second):
    x = tokens.reshape(LB, RB, CK * CM)

    def right_step(pair):
        return jnp.dot(pair[0], pair[1], preferred_element_type=jnp.float32).astype(jnp.bfloat16)

    first = lax.map(right_step, (right_blocks, x))
    turned = jnp.swapaxes(first, 0, 1)
    second = lax.map(right_step, (left_blocks, turned))
    hidden = jnp.swapaxes(second, 0, 1).reshape(LB * RB, CK * CM)
    gated = (tokens.astype(jnp.float32) * hidden.astype(jnp.float32)).astype(jnp.bfloat16)
    rows_blk = 1024
    pieces = gated.reshape((LB * RB) // rows_blk, rows_blk, CK * CM)

    def mix_one(block):
        return channel_mix((block, chan_first, chan_second))

    out = lax.map(mix_one, pieces)
    return out.reshape(LB * RB, CK * CM)
```

```python
import jax
import jax.numpy as jnp
from jax import lax
from jax.sharding import PartitionSpec as P

CHUNKS = 4


def on_device(devices, tokens, right_blocks, left_blocks, chan_first, chan_second):
    rows_a, block_len, _ = right_blocks.shape
    width = tokens.shape[1]
    count_k, count_m = chan_first.shape[0], chan_first.shape[1]
    own_b = left_blocks.shape[0]
    chunks = min(CHUNKS, own_b)
    part = own_b // chunks
    blocks = left_blocks.shape[1]
    mix = (
        chan_first.transpose(0, 2, 1)[:, :, None, :].astype(jnp.float32)
        * chan_second.transpose(2, 1, 0)[:, None, :, :].astype(jnp.float32)
    ).astype(jnp.bfloat16).reshape(width, width)
    x = tokens.reshape(rows_a, block_len, width)
    right = right_blocks.reshape(rows_a, devices, chunks, part, block_len)
    left = left_blocks.reshape(chunks, part, blocks, blocks)
    pieces = tokens.reshape(rows_a, devices, chunks, part, width)
    outs = []
    for j in range(chunks):
        first = jnp.einsum(
            "adib,abc->diac", right[:, :, j], x, preferred_element_type=jnp.float32
        ).astype(jnp.bfloat16)
        got = lax.all_to_all(first, "seq", split_axis=0, concat_axis=0, tiled=True)
        second = jnp.einsum(
            "ixsa,siac->xic",
            left[j].reshape(part, blocks, devices, rows_a),
            got,
            preferred_element_type=jnp.float32,
        ).astype(jnp.bfloat16)
        back = lax.all_to_all(
            second.reshape(devices, rows_a, part, width), "seq", split_axis=0, concat_axis=0, tiled=True
        )
        hidden = jnp.swapaxes(back, 0, 1)
        gated = (pieces[:, :, j].astype(jnp.float32) * hidden.astype(jnp.float32)).astype(jnp.bfloat16)
        outs.append(
            jnp.dot(gated.reshape(-1, width), mix, preferred_element_type=jnp.float32)
            .astype(jnp.bfloat16)
            .reshape(rows_a, devices, part, width)
        )
    return jnp.stack(outs, axis=2).reshape(rows_a * block_len, width)


def solution(mesh):
    devices = mesh.shape["seq"]

    def run(*args):
        return on_device(devices, *args)

    return jax.shard_map(
        run,
        mesh=mesh,
        in_specs=(P(("groups", "seq"), None), P("seq", None, None), P("seq", None, None), P(), P()),
        out_specs=P(("groups", "seq"), None),
        check_vma=False,
    )
```

```python
import jax
import jax.numpy as jnp
from jax import lax
from jax.experimental import pallas as pl
from jax.experimental.pallas import tpu as pltpu
from jax.sharding import PartitionSpec as P


def chunk_list(own_b):
    if own_b % 32 == 0:
        quarter = own_b // 4
        return [(0, quarter), (2 * quarter, 2 * quarter), (quarter, quarter)]
    return [(0, own_b)]


def gate_mix(tokens, hidden, mix, out, start, rows_step):
    rows_a, devices, _, width = tokens.shape
    part = hidden.shape[2]
    rows = rows_step * devices * part

    def kernel(tokens_ref, hidden_ref, mix_ref, *refs):
        out_ref = refs[-1]
        for r in range(rows_step):
            gated = tokens_ref[r].astype(jnp.float32) * hidden_ref[:, r].astype(jnp.float32)
            gated = gated.reshape(rows // rows_step, width).astype(jnp.bfloat16)
            res = jnp.dot(gated, mix_ref[...], preferred_element_type=jnp.float32)
            out_ref[r] = res.reshape(devices, part, width).astype(jnp.bfloat16)

    own = pl.BlockSpec((rows_step, devices, part, width), lambda a: (a, 0, start // part, 0))
    in_specs = [
        own,
        pl.BlockSpec((devices, rows_step, part, width), lambda a: (0, a, 0, 0)),
        pl.BlockSpec((width, width), lambda a: (0, 0)),
    ]
    operands = [tokens, hidden, mix]
    aliases = {}
    if out is not None:
        in_specs.append(pl.BlockSpec(memory_space=pl.ANY))
        operands.append(out)
        aliases = {3: 0}
    total = rows_a * devices * part
    return pl.pallas_call(
        kernel,
        grid=(rows_a // rows_step,),
        in_specs=in_specs,
        out_specs=own,
        out_shape=jax.ShapeDtypeStruct(tokens.shape, jnp.bfloat16),
        input_output_aliases=aliases,
        compiler_params=pltpu.CompilerParams(vmem_limit_bytes=56 * 2**20),
        cost_estimate=pl.CostEstimate(
            flops=2 * total * width * width,
            bytes_accessed=6 * total * width + 2 * width * width,
            transcendentals=0,
        ),
        name="gate_mix",
    )(*operands)


def on_device(devices, tokens, right_blocks, left_blocks, chan_first, chan_second):
    rows_a, block_len, _ = right_blocks.shape
    width = tokens.shape[1]
    own_b = left_blocks.shape[0]
    blocks = left_blocks.shape[1]
    mix = (
        chan_first.transpose(0, 2, 1)[:, :, None, :].astype(jnp.float32)
        * chan_second.transpose(2, 1, 0)[:, None, :, :].astype(jnp.float32)
    ).astype(jnp.bfloat16).reshape(width, width)
    x = tokens.reshape(rows_a, block_len, width)
    right = right_blocks.reshape(rows_a, devices, own_b, block_len)
    pieces = tokens.reshape(rows_a, devices, own_b, width)
    out = None
    for start, part in chunk_list(own_b):
        first = jnp.einsum(
            "adib,abc->diac", right[:, :, start : start + part], x, preferred_element_type=jnp.float32
        ).astype(jnp.bfloat16)
        got = lax.all_to_all(first, "seq", split_axis=0, concat_axis=0, tiled=True)
        second = jnp.einsum(
            "ixsa,siac->xic",
            left_blocks[start : start + part].reshape(part, blocks, devices, rows_a),
            got,
            preferred_element_type=jnp.float32,
        ).astype(jnp.bfloat16)
        back = lax.all_to_all(
            second.reshape(devices, rows_a, part, width), "seq", split_axis=0, concat_axis=0, tiled=True
        )
        if part % 8 == 0:
            rows_step = 2 if part == 8 and rows_a % 2 == 0 else 1
            out = gate_mix(pieces, back, mix, out, start, rows_step)
        else:
            hidden = jnp.swapaxes(back, 0, 1)
            gated = (pieces.astype(jnp.float32) * hidden.astype(jnp.float32)).astype(jnp.bfloat16)
            out = jnp.dot(gated.reshape(-1, width), mix, preferred_element_type=jnp.float32).astype(
                jnp.bfloat16
            )
    return out.reshape(rows_a * block_len, width)


def solution(mesh):
    devices = mesh.shape["seq"]

    def run(*args):
        return on_device(devices, *args)

    return jax.shard_map(
        run,
        mesh=mesh,
        in_specs=(P(("groups", "seq"), None), P("seq", None, None), P("seq", None, None), P(), P()),
        out_specs=P(("groups", "seq"), None),
        check_vma=False,
    )
```
